512 devices in a mesh: gx: 32 (over z, x_lo), gy: 16 (over x_hi, y, core).
Axes of the slice: x: 4 (x_hi: 2, x_lo: 2; x = x_hi * 2 + x_lo), y: 4, z: 16, core: 2. Of those that a mesh axis runs over, the one named last changes fastest.
Arguments:
- adjoint_forcing: float32 [4, 6, 1024, 4096], P(None, None, 'gx', 'gy'), may hold values from -6 to 6
- field_mixing: float32 [4, 4], replicated, may hold values from -3 to 3
- time_mixing: float32 [6, 6], replicated, may hold values from -2.5 to 2.5
- kernel_east: float32 [21], replicated, may hold values from 0.1 to 1
- kernel_north: float32 [21], replicated, may hold values from 0.1 to 1
- spatial_modes: bfloat16 [1024, 4096, 256], P('gx', 'gy'), may hold values from -0.00390625 to 0.00390625
- coefficients: float32 [256, 24], P('gy'), may hold values from -6 to 6
Outputs:
- gradient: float32 [256, 24], P('gy')
The draws below stay inside these ranges and needn't reach their ends.
All inputs are finite; a program needn't handle non-finite values.
Results may differ from the reference program's by a relative error of at most 0.0029.
Values sent between devices are 32-bit elements; how exact they have to be, the bound alone decides.
A program may use at most 64 MiB of HBM per device.

```python
import jax
import jax.numpy as jnp
from jax import lax

FIELDS = 4
LEVELS = 6
MODES = 256
RADIUS = 10
NX = 1024
NY = 4096


def spiked(result, stream_key, source, target, blocks, factor):
    owner, partner = [(jnp.arange(result.shape[position]) // (result.shape[position] // blocks)).reshape([-1 if axis == position else 1 for axis in range(result.ndim)]) for position in (source, target)]
    chosen = jax.random.permutation(stream_key, blocks)[partner]
    strong = (owner == chosen) | (owner == (partner + blocks // 2) % blocks)
    return jnp.where(strong, factor * result, result)


def block_levels(stream_key, extent, shards, least, high):
    gain, own = 1.0, jax.random.fold_in(stream_key, 6)
    for axis_at, shards_of in shards:
        draws = jnp.exp(jax.random.uniform(jax.random.fold_in(own, axis_at), (shards_of,), jnp.float32, least / len(shards), high / len(shards)))
        gain = gain * jnp.repeat(draws, extent[axis_at] // shards_of).reshape([-1 if axis == axis_at else 1 for axis in range(len(extent))])
    return gain


def bell_draw(key, extent, spread, limit, pieces=(), dtype=jnp.bfloat16):
    level = block_levels(key, extent, pieces, -0.22, 0.18) if pieces else 1.0
    values = jax.random.normal(key, extent, jnp.float32) * spread * level
    return jnp.minimum(jnp.maximum(values, -limit), limit).astype(dtype)


def bell_draw_with(key, dims, width, limit, shards, heavy, held_as=jnp.bfloat16):
    values = width * jax.random.normal(key, dims, jnp.float32)
    if shards:
        values = values * block_levels(key, dims, shards, -0.22, 0.18)
    return jnp.clip(spiked(values, jax.random.fold_in(key, 3), *heavy), -limit, limit).astype(held_as)


def setup_inputs(seed: int = 0) -> dict:
    streams_of = jax.random.split(jax.random.key(seed), 8)
    adjoint_forcing = bell_draw(streams_of[0], (FIELDS, LEVELS, NX, NY), 1.0, 6.0, ((2, 32), (3, 16)), jnp.float32)
    field_mixing = bell_draw(streams_of[1], (FIELDS, FIELDS), FIELDS ** -0.5, 3.0, (), jnp.float32)
    time_mixing = bell_draw(streams_of[2], (LEVELS, LEVELS), LEVELS ** -0.5, 2.5, (), jnp.float32)
    kernel_east = jnp.clip(jax.random.uniform(streams_of[3], (2 * RADIUS + 1,), jnp.float32, 0.1, 1.0), 0.1, 1.0)
    kernel_north = jnp.clip(jax.random.uniform(streams_of[4], (2 * RADIUS + 1,), jnp.float32, 0.1, 1.0), 0.1, 1.0)
    spatial_modes = bell_draw_with(streams_of[5], (NX, NY, MODES), (NX * NY) ** -0.5, 0.00390625, ((0, 32), (1, 16)), (1, 2, 16, 2.0))
    coefficients = bell_draw(streams_of[6], (MODES, FIELDS * LEVELS), 1.0, 6.0, ((0, 16),), jnp.float32)
    return {"adjoint_forcing": adjoint_forcing, "field_mixing": field_mixing, "time_mixing": time_mixing, "kernel_east": kernel_east, "kernel_north": kernel_north, "spatial_modes": spatial_modes, "coefficients": coefficients}


def smooth(field, taps, axis, reach):
    count = field.shape[axis]
    pads = [(0, 0)] * field.ndim
    pads[axis] = (reach, reach)
    padded = jnp.pad(field, pads)
    total = jnp.zeros(field.shape, jnp.float32)
    for j in range(2 * reach + 1):
        total = total + taps[j] * lax.slice_in_dim(padded, j, j + count, axis=axis)
    return total


def reference(adjoint_forcing, field_mixing, time_mixing, kernel_east, kernel_north, spatial_modes, coefficients):
    mixed = jnp.einsum("gf,st,gsxy->ftxy", field_mixing, time_mixing, adjoint_forcing, precision=lax.Precision.HIGHEST)
    along_x = smooth(mixed, kernel_east, 2, RADIUS)
    smoothed = smooth(along_x, kernel_north, 3, RADIUS).astype(jnp.bfloat16)
    flat_state = smoothed.reshape(FIELDS * LEVELS, NX * NY)
    flat_modes = spatial_modes.reshape(NX * NY, MODES)
    projection = lax.dot_general(flat_modes, flat_state, (((0,), (1,)), ((), ())), preferred_element_type=jnp.float32)
    return coefficients + projection
```

```python
import functools

import jax
import jax.numpy as jnp
from jax import lax
from jax.experimental import pallas as pl
from jax.experimental.pallas import tpu as pltpu
from jax.sharding import PartitionSpec as P

F32, BF16 = jnp.float32, jnp.bfloat16
MESH = pl.DeviceIdType.MESH
C = 24
WX, WY = 32, 256
R = 10
TAPS = 2 * R + 1
MODES = 256
LANES = 128
SLAB = 384
ROW = C
CHUNKS = ((0, 4), (4, 3), (7, 3))


def dot(a, b):
    return jnp.dot(a, b, preferred_element_type=F32)


def split(a):
    high = a.astype(BF16)
    return high, (a - high.astype(F32)).astype(BF16)


def dot3(a, b_high, b_low):
    high, low = split(a)
    return dot(high, b_high) + (dot(high, b_low) + dot(low, b_high))


def iota(shape, dim):
    return lax.broadcasted_iota(jnp.int32, shape, dim)


def band(taps, row0, shift, shape):
    index = iota(shape, 0) - iota(shape, 1) + (row0 + shift)
    out = jnp.zeros(shape, F32)
    for j in range(TAPS):
        out = jnp.where(index == j, taps[j], out)
    return out


def kernel(
    nx, ny,
    adj_hbm, fm_hbm, tm_hbm, ke_hbm, kn_hbm, modes_hbm,
    out_ref,
    adj, modes, fm, tm, ke, kn,
    t_high, t_low, e_high, e_low, y0, ext, part,
    pack_s, pack_r, z_high, z_low, slabs, got_y, got_x,
    load_sem, ysend, yrecv, xsend, xrecv, rs_send, rs_recv, ag_send, ag_recv,
):
    gx, gy = lax.axis_index("gx"), lax.axis_index("gy")
    copy_adj = pltpu.make_async_copy(adj_hbm, adj, load_sem.at[0])
    copy_kn = pltpu.make_async_copy(kn_hbm, kn, load_sem.at[1])
    copy_ke = pltpu.make_async_copy(ke_hbm, ke, load_sem.at[2])
    copy_fm = pltpu.make_async_copy(fm_hbm, fm, load_sem.at[3])
    copy_tm = pltpu.make_async_copy(tm_hbm, tm, load_sem.at[4])
    copy_modes = pltpu.make_async_copy(modes_hbm, modes, load_sem.at[5])
    for copy in (copy_adj, copy_kn, copy_ke, copy_fm, copy_tm, copy_modes):
        copy.start()

    barrier = pltpu.get_barrier_semaphore()

    @pl.loop(1, ny)
    def _(d):
        pl.semaphore_signal(
            barrier, inc=1, device_id={"gy": lax.rem(gy + d, ny)}, device_id_type=MESH
        )

    @pl.loop(1, nx)
    def _(d):
        pl.semaphore_signal(
            barrier, inc=1, device_id={"gx": lax.rem(gx + d, nx)}, device_id_type=MESH
        )

    copy_kn.wait()
    for i in range(0, WY, 16):
        for h in range(0, WY, LANES):
            rows = (pl.ds(i, 16), pl.ds(h, LANES))
            if i - R > h + LANES - 1 or i + 15 + R < h:
                t_high[rows] = jnp.zeros((16, LANES), BF16)
                t_low[rows] = jnp.zeros((16, LANES), BF16)
            else:
                t_high[rows], t_low[rows] = split(band(kn, i - h, R, (16, LANES)))
    zeros = jnp.zeros((16, LANES), BF16)
    edge_row = iota((16, LANES), 0) < R
    e_high[...] = jnp.zeros_like(e_high)
    e_low[...] = jnp.zeros_like(e_low)
    low_side = jnp.where(edge_row, band(kn, 0, 0, (16, LANES)), 0.0)
    e_high[0:16, 0:LANES], e_low[0:16, 0:LANES] = split(low_side)
    high_side = jnp.where(edge_row, band(kn, WY - LANES, R, (16, LANES)), 0.0)
    e_high[16:32, LANES:WY], e_low[16:32, LANES:WY] = split(high_side)

    copy_adj.wait()
    lane = iota((64, LANES), 1)
    pack_low = jnp.zeros((64, LANES), F32)
    pack_high = jnp.zeros((64, LANES), F32)
    for b in range(12):
        here = (lane >= R * b) & (lane < R * (b + 1))
        low = adj[2 * b : 2 * b + 2, :, 0:LANES].reshape(64, LANES)
        high = adj[2 * b : 2 * b + 2, :, LANES:WY].reshape(64, LANES)
        if b:
            low = pltpu.roll(low, R * b, 1)
        high = pltpu.roll(high, (R * b + R) % LANES, 1)
        pack_low = jnp.where(here, low, pack_low)
        pack_high = jnp.where(here, high, pack_high)
    pack_s[0] = pack_low
    pack_s[1] = pack_high

    pl.semaphore_wait(barrier, nx + ny - 2)

    to_south = pltpu.make_async_remote_copy(
        pack_s.at[0], pack_r.at[1], ysend.at[0], yrecv.at[1],
        device_id={"gy": jnp.maximum(gy - 1, 0)}, device_id_type=MESH,
    )
    to_north = pltpu.make_async_remote_copy(
        pack_s.at[1], pack_r.at[0], ysend.at[1], yrecv.at[0],
        device_id={"gy": jnp.minimum(gy + 1, ny - 1)}, device_id_type=MESH,
    )

    @pl.when(gy > 0)
    def _():
        to_south.start()

    @pl.when(gy < ny - 1)
    def _():
        to_north.start()

    for q in range(3):
        tile = adj[8 * q : 8 * q + 8].reshape(256, WY)
        y0[256 * q : 256 * q + 256, :] = dot3(tile, t_high[...], t_low[...])

    @pl.when(gy > 0)
    def _():
        to_north.wait_recv()

    @pl.when(gy == 0)
    def _():
        pack_r[0] = jnp.zeros((64, LANES), F32)

    @pl.when(gy < ny - 1)
    def _():
        to_south.wait_recv()

    @pl.when(gy == ny - 1)
    def _():
        pack_r[1] = jnp.zeros((64, LANES), F32)

    from_low, from_high = pack_r[0], pack_r[1]
    for q in range(3):
        pieces = []
        for b in range(4 * q, 4 * q + 4):
            low = pltpu.roll(from_low, (LANES - R * b) % LANES, 1) if b else from_low
            high = pltpu.roll(from_high, (LANES + 16 - R * b) % LANES, 1)
            pieces.append(jnp.where(lane < 16, low, high))
        extra = jnp.concatenate(pieces, axis=0)
        total = y0[256 * q : 256 * q + 256, :] + dot3(extra, e_high[...], e_low[...])
        for c in range(8):
            rows = pl.ds(R * ROW + 8 * q + c, WX, stride=ROW)
            ext[0, rows, :] = total[32 * c : 32 * c + 32, :LANES]
            ext[1, rows, :] = total[32 * c : 32 * c + 32, LANES:]

    west, east = jnp.maximum(gx - 1, 0), jnp.minimum(gx + 1, nx - 1)
    to_west, to_east = [], []
    for k, (first, count) in enumerate(CHUNKS):
        rows = count * ROW
        to_west.append(
            pltpu.make_async_remote_copy(
                ext.at[:, pl.ds((R + first) * ROW, rows)],
                ext.at[:, pl.ds((R + WX + first) * ROW, rows)],
                xsend.at[k], xrecv.at[k],
                device_id={"gx": west}, device_id_type=MESH,
            )
        )
        to_east.append(
            pltpu.make_async_remote_copy(
                ext.at[:, pl.ds((R + WX - first - count) * ROW, rows)],
                ext.at[:, pl.ds((R - first - count) * ROW, rows)],
                xsend.at[3 + k], xrecv.at[3 + k],
                device_id={"gx": east}, device_id_type=MESH,
            )
        )
    for k in range(len(CHUNKS)):

        @pl.when(gx > 0)
        def _():
            to_west[k].start()

        @pl.when(gx < nx - 1)
        def _():
            to_east[k].start()

    copy_fm.wait()
    copy_tm.wait()
    copy_ke.wait()
    row, col = iota((C, LANES), 0), iota((C, LANES), 1)
    field_part = jnp.zeros((C, LANES), F32)
    for g in range(4):
        for f in range(4):
            chosen = (row // 6 == g) & (col // 6 == f)
            field_part = jnp.where(chosen, fm[g, f], field_part)
    time_part = jnp.zeros((C, LANES), F32)
    for s in range(6):
        for t in range(6):
            chosen = (row % 6 == s) & (col % 6 == t)
            time_part = jnp.where(chosen, tm[s, t], time_part)
    mix = field_part * time_part
    group = lax.rem(gy, 8)
    lane_of = iota((SLAB, C), 0)
    channel = 8 * (lane_of // LANES) + lax.rem(group + 8 - (lane_of % LANES) // 16, 8)
    pick = (channel == iota((SLAB, C), 1)).astype(F32)
    mixing = jnp.dot(pick, mix, preferred_element_type=F32, precision=lax.Precision.HIGHEST)
    z_high[...], z_low[...] = split(mixing)

    def column(start):
        return jnp.concatenate([ext[h, pl.ds(start, ROW), :] for h in range(2)], axis=1)

    def columns(start, count, first_tap):
        total = ke[first_tap] * column(start)
        for j in range(1, count):
            total = total + ke[first_tap + j] * column(start + j * ROW)
        return total

    def project(total, x):
        low = total - total.astype(BF16).astype(F32)
        both = jnp.concatenate([total, low], axis=0).astype(BF16)
        return dot(both, modes[x])

    copy_modes.wait()

    def interior(x, acc):
        start = pl.multiple_of(x * ROW, 8)
        return acc + project(columns(start, TAPS, 0), x)

    acc = lax.fori_loop(R, WX - R, interior, jnp.zeros((2 * C, MODES), F32))

    for e in range(R):
        part[e] = columns(R * ROW, e + R + 1, R - e)
        part[R + e] = columns((WX - 1 - e) * ROW, e + R + 1, 0)

    @pl.when(gx == 0)
    def _():
        ext[:, 0 : R * ROW, :] = jnp.zeros((2, R * ROW, LANES), F32)

    @pl.when(gx == nx - 1)
    def _():
        ext[:, (R + WX) * ROW : (2 * R + WX) * ROW, :] = jnp.zeros((2, R * ROW, LANES), F32)

    for k, (first, count) in enumerate(CHUNKS):

        @pl.when(gx > 0)
        def _():
            to_east[k].wait_recv()

        @pl.when(gx < nx - 1)
        def _():
            to_west[k].wait_recv()

        last = first + count
        for e in range(R - first):
            low, high = part[e], part[R + e]
            for d in range(first + 1, min(last, R - e) + 1):
                low = low + ke[R - d - e] * column((R - d) * ROW)
                high = high + ke[R + d + e] * column((R + WX - 1 + d) * ROW)
            if R - e <= last:
                acc = acc + project(low, e)
                acc = acc + project(high, WX - 1 - e)
            else:
                part[e] = low
                part[R + e] = high

    total = acc[:C] + acc[C:]

    sub, lanes = iota((8, LANES), 0), iota((8, LANES), 1) // 16
    for r in range(3):
        for h in range(2):
            v = total[8 * r : 8 * r + 8, LANES * h : LANES * h + LANES]
            for bit in (1, 2, 4):
                v = jnp.where((sub & bit) != 0, pltpu.roll(v, LANES - 16 * bit, 1), v)
            for bit in (1, 2, 4):
                v = jnp.where((lanes & bit) != 0, pltpu.roll(v, bit, 0), v)
            for g in range(8):
                slabs[8 * h + g, :, LANES * r : LANES * r + LANES] = v[g : g + 1]

    @pl.loop(1, ny)
    def _(d):
        peer = lax.rem(gy + d, ny)
        pltpu.make_async_remote_copy(
            slabs.at[peer], got_y.at[d - 1], rs_send, rs_recv,
            device_id={"gy": peer}, device_id_type=MESH,
        ).start()

    mine = slabs[gy]
    pltpu.make_async_copy(got_y, got_y, rs_recv).wait()
    for d in range(ny - 1):
        mine = mine + got_y[d]
    got_x[gx] = mine

    @pl.loop(1, nx)
    def _(d):
        peer = lax.rem(gx + d, nx)
        pltpu.make_async_remote_copy(
            got_x.at[gx], got_x.at[gx], ag_send, ag_recv,
            device_id={"gx": peer}, device_id_type=MESH,
        ).start()

    others = got_x.at[pl.ds(0, nx - 1)]
    pltpu.make_async_copy(others, others, ag_recv).wait()
    whole = got_x[0]
    for d in range(1, nx):
        whole = whole + got_x[d]

    shape = (16, SLAB)
    spread = jnp.where(
        iota(shape, 1) % 16 == iota(shape, 0), jnp.broadcast_to(whole, shape), 0.0
    )
    out_ref[...] = dot3(spread, z_high[...], z_low[...])[:, :C]

    @pl.when(gy > 0)
    def _():
        to_south.wait_send()

    @pl.when(gy < ny - 1)
    def _():
        to_north.wait_send()

    for k in range(len(CHUNKS)):

        @pl.when(gx > 0)
        def _():
            to_west[k].wait_send()

        @pl.when(gx < nx - 1)
        def _():
            to_east[k].wait_send()

    pltpu.make_async_copy(got_y, got_y, rs_send).wait()
    pltpu.make_async_copy(others, others, ag_send).wait()


def solution(mesh):
    nx, ny = mesh.shape["gx"], mesh.shape["gy"]

    def local(adj, field_mixing, time_mixing, kernel_east, kernel_north, modes, coefficients):
        vmem, smem, dma = pltpu.VMEM, pltpu.SMEM, pltpu.SemaphoreType.DMA
        projection = pl.pallas_call(
            functools.partial(kernel, nx, ny),
            out_shape=jax.ShapeDtypeStruct((MODES // ny, C), F32),
            in_specs=[pl.BlockSpec(memory_space=pl.ANY)] * 6,
            out_specs=pl.BlockSpec(memory_space=pltpu.VMEM),
            scratch_shapes=[
                vmem((C, WX, WY), F32),
                vmem((WX, WY, MODES), BF16),
                smem((4, 4), F32),
                smem((6, 6), F32),
                smem((TAPS,), F32),
                smem((TAPS,), F32),
                vmem((WY, WY), BF16),
                vmem((WY, WY), BF16),
                vmem((LANES, WY), BF16),
                vmem((LANES, WY), BF16),
                vmem((C * WX, WY), F32),
                vmem((2, (WX + 2 * R) * ROW, LANES), F32),
                vmem((2 * R, C, WY), F32),
                vmem((2, 64, LANES), F32),
                vmem((2, 64, LANES), F32),
                vmem((SLAB, LANES), BF16),
                vmem((SLAB, LANES), BF16),
                vmem((ny, 1, SLAB), F32),
                vmem((ny - 1, 1, SLAB), F32),
                vmem((nx, 1, SLAB), F32),
                dma((6,)),
                dma((2,)),
                dma((2,)),
                dma((6,)),
                dma((6,)),
                dma,
                dma,
                dma,
                dma,
            ],
            compiler_params=pltpu.CompilerParams(
                collective_id=0, has_side_effects=True, vmem_limit_bytes=40 << 20
            ),
            name="gradient",
        )(
            adj.reshape(C, WX, WY), field_mixing, time_mixing,
            kernel_east, kernel_north, modes,
        )
        return coefficients + projection

    in_specs = (P(None, None, "gx", "gy"), P(), P(), P(), P(), P("gx", "gy", None), P("gy", None))
    return jax.shard_map(
        local, mesh=mesh, in_specs=in_specs, out_specs=P("gy", None), check_vma=False
    )
```

```python
import functools

import jax
import jax.numpy as jnp
from jax import lax
from jax.experimental import pallas as pl
from jax.experimental.pallas import tpu as pltpu
from jax.sharding import PartitionSpec as P

F32, BF16 = jnp.float32, jnp.bfloat16
MESH = pl.DeviceIdType.MESH
C = 24
WX, WY = 32, 256
R = 10
TAPS = 2 * R + 1
MODES = 256
LANES = 128
SLAB = 384
ROW = C
NEAR = 4
CHUNKS = ((0, NEAR), (4, 3), (7, 3))


def dot(a, b):
    return jnp.dot(a, b, preferred_element_type=F32)


def split(a):
    high = a.astype(BF16)
    return high, (a - high.astype(F32)).astype(BF16)


def dot3(a, b_high, b_low):
    high, low = split(a)
    return dot(high, b_high) + (dot(high, b_low) + dot(low, b_high))


def iota(shape, dim):
    return lax.broadcasted_iota(jnp.int32, shape, dim)


def band(taps, row0, shift, shape):
    index = iota(shape, 0) - iota(shape, 1) + (row0 + shift)
    out = jnp.zeros(shape, F32)
    for j in range(TAPS):
        out = jnp.where(index == j, taps[j], out)
    return out


def kernel(
    nx, ny,
    adj_hbm, fm_hbm, tm_hbm, ke_hbm, kn_hbm, modes_hbm,
    out_ref,
    adj, modes, fm, tm, ke, kn,
    t_high, t_low, e_high, e_low, y0, ext, part,
    pack_s, pack_r, raw_s, raw_r, corner_s, corner_r, z_high, z_low, slabs, got_y, got_x,
    load_sem, ysend, yrecv, xsend, xrecv, csend, crecv, rs_send, rs_recv, ag_send, ag_recv,
):
    gx, gy = lax.axis_index("gx"), lax.axis_index("gy")
    copy_adj = pltpu.make_async_copy(adj_hbm, adj, load_sem.at[0])
    copy_kn = pltpu.make_async_copy(kn_hbm, kn, load_sem.at[1])
    copy_ke = pltpu.make_async_copy(ke_hbm, ke, load_sem.at[2])
    copy_fm = pltpu.make_async_copy(fm_hbm, fm, load_sem.at[3])
    copy_tm = pltpu.make_async_copy(tm_hbm, tm, load_sem.at[4])
    copy_modes = pltpu.make_async_copy(modes_hbm, modes, load_sem.at[5])
    for copy in (copy_adj, copy_kn, copy_ke, copy_fm, copy_tm):
        copy.start()

    barrier = pltpu.get_barrier_semaphore()

    def greet(there):
        pl.semaphore_signal(barrier, inc=1, device_id=there, device_id_type=MESH)

    west, east = jnp.maximum(gx - 1, 0), jnp.minimum(gx + 1, nx - 1)
    south, north = jnp.maximum(gy - 1, 0), jnp.minimum(gy + 1, ny - 1)
    has_x = (gx > 0, gx < nx - 1)
    has_y = (gy > 0, gy < ny - 1)
    diagonal = [
        (2 * i + j, has_x[i] & has_y[j], {"gx": (west, east)[i], "gy": (south, north)[j]})
        for i in range(2)
        for j in range(2)
    ]
    for d in range(1, nx):
        greet({"gx": gx ^ d})
    for d in range(1, ny):
        greet({"gy": gy ^ d})
    greeted = nx + ny - 2
    for i, there, device in diagonal:

        @pl.when(there)
        def _():
            greet(device)

        greeted = greeted + there.astype(jnp.int32)

    copy_kn.wait()
    for i in range(0, WY, 16):
        for h in range(0, WY, LANES):
            rows = (pl.ds(i, 16), pl.ds(h, LANES))
            if i - R > h + LANES - 1 or i + 15 + R < h:
                t_high[rows] = jnp.zeros((16, LANES), BF16)
                t_low[rows] = jnp.zeros((16, LANES), BF16)
            else:
                t_high[rows], t_low[rows] = split(band(kn, i - h, R, (16, LANES)))
    edge_row = iota((16, LANES), 0) < R
    e_high[...] = jnp.zeros_like(e_high)
    e_low[...] = jnp.zeros_like(e_low)
    low_side = jnp.where(edge_row, band(kn, 0, 0, (16, LANES)), 0.0)
    e_high[0:16, 0:LANES], e_low[0:16, 0:LANES] = split(low_side)
    high_side = jnp.where(edge_row, band(kn, WY - LANES, R, (16, LANES)), 0.0)
    e_high[16:32, LANES:WY], e_low[16:32, LANES:WY] = split(high_side)

    copy_adj.wait()
    copy_modes.start()
    lane = iota((64, LANES), 1)
    pack_low = jnp.zeros((64, LANES), F32)
    pack_high = jnp.zeros((64, LANES), F32)
    for b in range(12):
        here = (lane >= R * b) & (lane < R * (b + 1))
        low = adj[2 * b : 2 * b + 2, :, 0:LANES].reshape(64, LANES)
        high = adj[2 * b : 2 * b + 2, :, LANES:WY].reshape(64, LANES)
        if b:
            low = pltpu.roll(low, R * b, 1)
        high = pltpu.roll(high, (R * b + R) % LANES, 1)
        pack_low = jnp.where(here, low, pack_low)
        pack_high = jnp.where(here, high, pack_high)
    pack_s[0] = pack_low
    pack_s[1] = pack_high

    pl.semaphore_wait(barrier, greeted)

    to_south = pltpu.make_async_remote_copy(
        pack_s.at[0], pack_r.at[1], ysend.at[0], yrecv.at[1],
        device_id={"gy": south}, device_id_type=MESH,
    )
    to_north = pltpu.make_async_remote_copy(
        pack_s.at[1], pack_r.at[0], ysend.at[1], yrecv.at[0],
        device_id={"gy": north}, device_id_type=MESH,
    )

    @pl.when(gy > 0)
    def _():
        to_south.start()

    @pl.when(gy < ny - 1)
    def _():
        to_north.start()

    for side, first in enumerate((0, WX - 8)):
        for c in range(C):
            edge = adj[c, first : first + 8, :]
            for h in range(2):
                raw_s[side, h, pl.ds(c, 8, stride=ROW), :] = edge[:, LANES * h : LANES * h + LANES]

    near = NEAR * ROW
    raw_west = pltpu.make_async_remote_copy(
        raw_s.at[0, :, pl.ds(0, near)], raw_r.at[1], xsend.at[0], xrecv.at[0],
        device_id={"gx": west}, device_id_type=MESH,
    )
    raw_east = pltpu.make_async_remote_copy(
        raw_s.at[1, :, pl.ds(near, near)], raw_r.at[0], xsend.at[3], xrecv.at[3],
        device_id={"gx": east}, device_id_type=MESH,
    )

    @pl.when(gx > 0)
    def _():
        raw_west.start()

    @pl.when(gx < nx - 1)
    def _():
        raw_east.start()

    lane8 = iota((8, LANES), 1)
    corners = []
    for i in range(2):
        for j in range(2):
            packed = jnp.zeros((8, LANES), F32)
            for b in range(12):
                piece = raw_s[i, j, near * i + 8 * b : near * i + 8 * b + 8, :]
                piece = pltpu.roll(piece, (R * b + R * j) % LANES, 1) if b + j else piece
                packed = jnp.where((lane8 >= R * b) & (lane8 < R * (b + 1)), piece, packed)
            corner_s[2 * i + j] = packed
    for k, there, device in diagonal:
        copy = pltpu.make_async_remote_copy(
            corner_s.at[k], corner_r.at[3 - k], csend.at[k], crecv.at[3 - k],
            device_id=device, device_id_type=MESH,
        )
        corners.append(copy)

        @pl.when(there)
        def _():
            copy.start()

    for q in range(3):
        tile = adj[8 * q : 8 * q + 8].reshape(256, WY)
        y0[256 * q : 256 * q + 256, :] = dot3(tile, t_high[...], t_low[...])

    @pl.when(gy > 0)
    def _():
        to_north.wait_recv()

    @pl.when(gy == 0)
    def _():
        pack_r[0] = jnp.zeros((64, LANES), F32)

    @pl.when(gy < ny - 1)
    def _():
        to_south.wait_recv()

    @pl.when(gy == ny - 1)
    def _():
        pack_r[1] = jnp.zeros((64, LANES), F32)

    from_low, from_high = pack_r[0], pack_r[1]
    for q in range(3):
        pieces = []
        for b in range(4 * q, 4 * q + 4):
            low = pltpu.roll(from_low, (LANES - R * b) % LANES, 1) if b else from_low
            high = pltpu.roll(from_high, (LANES + 16 - R * b) % LANES, 1)
            pieces.append(jnp.where(lane < 16, low, high))
        extra = jnp.concatenate(pieces, axis=0)
        total = y0[256 * q : 256 * q + 256, :] + dot3(extra, e_high[...], e_low[...])
        for c in range(8):
            rows = pl.ds(R * ROW + 8 * q + c, WX, stride=ROW)
            ext[0, rows, :] = total[32 * c : 32 * c + 32, :LANES]
            ext[1, rows, :] = total[32 * c : 32 * c + 32, LANES:]

    to_west, to_east = [raw_west], [raw_east]
    for k, (first, count) in enumerate(CHUNKS):
        if not k:
            continue
        rows = count * ROW
        to_west.append(
            pltpu.make_async_remote_copy(
                ext.at[:, pl.ds((R + first) * ROW, rows)],
                ext.at[:, pl.ds((R + WX + first) * ROW, rows)],
                xsend.at[k], xrecv.at[k],
                device_id={"gx": west}, device_id_type=MESH,
            )
        )
        to_east.append(
            pltpu.make_async_remote_copy(
                ext.at[:, pl.ds((R + WX - first - count) * ROW, rows)],
                ext.at[:, pl.ds((R - first - count) * ROW, rows)],
                xsend.at[3 + k], xrecv.at[3 + k],
                device_id={"gx": east}, device_id_type=MESH,
            )
        )
    for k in range(1, len(CHUNKS)):

        @pl.when(gx > 0)
        def _():
            to_west[k].start()

        @pl.when(gx < nx - 1)
        def _():
            to_east[k].start()

    copy_fm.wait()
    copy_tm.wait()
    copy_ke.wait()
    row, col = iota((C, LANES), 0), iota((C, LANES), 1)
    field_part = jnp.zeros((C, LANES), F32)
    for g in range(4):
        for f in range(4):
            chosen = (row // 6 == g) & (col // 6 == f)
            field_part = jnp.where(chosen, fm[g, f], field_part)
    time_part = jnp.zeros((C, LANES), F32)
    for s in range(6):
        for t in range(6):
            chosen = (row % 6 == s) & (col % 6 == t)
            time_part = jnp.where(chosen, tm[s, t], time_part)
    mix = field_part * time_part
    group = lax.rem(gy, 8)
    lane_of = iota((SLAB, C), 0)
    channel = 8 * (lane_of // LANES) + lax.rem(group + 8 - (lane_of % LANES) // 16, 8)
    pick = (channel == iota((SLAB, C), 1)).astype(F32)
    mixing = jnp.dot(pick, mix, preferred_element_type=F32, precision=lax.Precision.HIGHEST)
    z_high[...], z_low[...] = split(mixing)

    def column(start):
        return jnp.concatenate([ext[h, pl.ds(start, ROW), :] for h in range(2)], axis=1)

    def columns(start, count, first_tap):
        total = ke[first_tap] * column(start)
        for j in range(1, count):
            total = total + ke[first_tap + j] * column(start + j * ROW)
        return total

    def project(total, x):
        low = total - total.astype(BF16).astype(F32)
        both = jnp.concatenate([total, low], axis=0).astype(BF16)
        return dot(both, modes[x])

    copy_modes.wait()

    def interior(x, acc):
        start = pl.multiple_of(x * ROW, 8)
        return acc + project(columns(start, TAPS, 0), x)

    acc = lax.fori_loop(R, WX - R, interior, jnp.zeros((2 * C, MODES), F32))

    for e in range(R):
        part[e] = columns(R * ROW, e + R + 1, R - e)
        part[R + e] = columns((WX - 1 - e) * ROW, e + R + 1, 0)

    @pl.when(gx == 0)
    def _():
        ext[:, 0 : R * ROW, :] = jnp.zeros((2, R * ROW, LANES), F32)

    @pl.when(gx == nx - 1)
    def _():
        ext[:, (R + WX) * ROW : (2 * R + WX) * ROW, :] = jnp.zeros((2, R * ROW, LANES), F32)

    for k, (first, count) in enumerate(CHUNKS):

        @pl.when(gx > 0)
        def _():
            to_east[k].wait_recv()

        @pl.when(gx < nx - 1)
        def _():
            to_west[k].wait_recv()

        if not k:
            for i, there, device in diagonal:

                @pl.when(there)
                def _():
                    corners[3 - i].wait_recv()

                @pl.when(jnp.logical_not(there))
                def _():
                    corner_r[i] = jnp.zeros((8, LANES), F32)

            for side in range(2):

                @pl.when(has_x[side])
                def _():
                    low, high = corner_r[2 * side], corner_r[2 * side + 1]
                    pieces = []
                    for b in range(12):
                        a = pltpu.roll(low, (LANES - R * b) % LANES, 1) if b else low
                        c = pltpu.roll(high, (LANES + 16 - R * b) % LANES, 1)
                        pieces.append(jnp.where(lane8 < 16, a, c))
                    extra = jnp.concatenate(pieces, axis=0)
                    tile = jnp.concatenate([raw_r[side, 0], raw_r[side, 1]], axis=1)
                    done = dot3(tile, t_high[...], t_low[...])
                    done = done + dot3(extra, e_high[...], e_low[...])
                    at = (R - NEAR) * ROW if side == 0 else (R + WX) * ROW
                    ext[0, pl.ds(at, near), :] = done[:, :LANES]
                    ext[1, pl.ds(at, near), :] = done[:, LANES:]

        last = first + count
        for e in range(R - first):
            low, high = part[e], part[R + e]
            for d in range(first + 1, min(last, R - e) + 1):
                low = low + ke[R - d - e] * column((R - d) * ROW)
                high = high + ke[R + d + e] * column((R + WX - 1 + d) * ROW)
            if R - e <= last:
                acc = acc + project(low, e)
                acc = acc + project(high, WX - 1 - e)
            else:
                part[e] = low
                part[R + e] = high

    total = acc[:C] + acc[C:]

    sub, lanes = iota((8, LANES), 0), iota((8, LANES), 1) // 16
    for r in range(3):
        for h in range(2):
            v = total[8 * r : 8 * r + 8, LANES * h : LANES * h + LANES]
            for bit in (1, 2, 4):
                v = jnp.where((sub & bit) != 0, pltpu.roll(v, LANES - 16 * bit, 1), v)
            for bit in (1, 2, 4):
                v = jnp.where((lanes & bit) != 0, pltpu.roll(v, bit, 0), v)
            for g in range(8):
                slabs[8 * h + g, :, LANES * r : LANES * r + LANES] = v[g : g + 1]

    for d in sorted(range(1, ny), key=lambda d: -2 * (d & 12).bit_count() - (d & 3).bit_count()):
        peer = gy ^ d
        pltpu.make_async_remote_copy(
            slabs.at[peer], got_y.at[d - 1], rs_send, rs_recv,
            device_id={"gy": peer}, device_id_type=MESH,
        ).start()

    mine = slabs[gy]
    pltpu.make_async_copy(got_y, got_y, rs_recv).wait()
    for d in range(ny - 1):
        mine = mine + got_y[d]
    got_x[gx] = mine

    for peer in range(nx):

        @pl.when(gx != peer)
        def _():
            pltpu.make_async_remote_copy(
                got_x.at[gx], got_x.at[gx], ag_send, ag_recv,
                device_id={"gx": peer}, device_id_type=MESH,
            ).start()

    others = got_x.at[pl.ds(0, nx - 1)]
    pltpu.make_async_copy(others, others, ag_recv).wait()
    whole = got_x[0]
    for d in range(1, nx):
        whole = whole + got_x[d]

    shape = (16, SLAB)
    spread = jnp.where(
        iota(shape, 1) % 16 == iota(shape, 0), jnp.broadcast_to(whole, shape), 0.0
    )
    out_ref[...] = dot3(spread, z_high[...], z_low[...])[:, :C]

    @pl.when(gy > 0)
    def _():
        to_south.wait_send()

    @pl.when(gy < ny - 1)
    def _():
        to_north.wait_send()

    for k in range(len(CHUNKS)):

        @pl.when(gx > 0)
        def _():
            to_west[k].wait_send()

        @pl.when(gx < nx - 1)
        def _():
            to_east[k].wait_send()

    for k, there, device in diagonal:

        @pl.when(there)
        def _():
            corners[k].wait_send()

    pltpu.make_async_copy(got_y, got_y, rs_send).wait()
    pltpu.make_async_copy(others, others, ag_send).wait()


def solution(mesh):
    nx, ny = mesh.shape["gx"], mesh.shape["gy"]

    def local(adj, field_mixing, time_mixing, kernel_east, kernel_north, modes, coefficients):
        vmem, smem, dma = pltpu.VMEM, pltpu.SMEM, pltpu.SemaphoreType.DMA
        projection = pl.pallas_call(
            functools.partial(kernel, nx, ny),
            out_shape=jax.ShapeDtypeStruct((MODES // ny, C), F32),
            in_specs=[pl.BlockSpec(memory_space=pltpu.HBM)] * 6,
            out_specs=pl.BlockSpec(memory_space=pltpu.VMEM),
            scratch_shapes=[
                vmem((C, WX, WY), F32),
                vmem((WX, WY, MODES), BF16),
                smem((4, 4), F32),
                smem((6, 6), F32),
                smem((TAPS,), F32),
                smem((TAPS,), F32),
                vmem((WY, WY), BF16),
                vmem((WY, WY), BF16),
                vmem((LANES, WY), BF16),
                vmem((LANES, WY), BF16),
                vmem((C * WX, WY), F32),
                vmem((2, (WX + 2 * R) * ROW, LANES), F32),
                vmem((2 * R, C, WY), F32),
                vmem((2, 64, LANES), F32),
                vmem((2, 64, LANES), F32),
                vmem((2, 2, 8 * ROW, LANES), F32),
                vmem((2, 2, NEAR * ROW, LANES), F32),
                vmem((4, 8, LANES), F32),
                vmem((4, 8, LANES), F32),
                vmem((SLAB, LANES), BF16),
                vmem((SLAB, LANES), BF16),
                vmem((ny, 1, SLAB), F32),
                vmem((ny - 1, 1, SLAB), F32),
                vmem((nx, 1, SLAB), F32),
                dma((6,)),
                dma((2,)),
                dma((2,)),
                dma((6,)),
                dma((6,)),
                dma((4,)),
                dma((4,)),
                dma,
                dma,
                dma,
                dma,
            ],
            compiler_params=pltpu.CompilerParams(
                collective_id=0, has_side_effects=True
            ),
            name="gradient",
        )(
            adj.reshape(C, WX, WY), field_mixing, time_mixing,
            kernel_east, kernel_north, modes,
        )
        return coefficients + projection

    in_specs = (P(None, None, "gx", "gy"), P(), P(), P(), P(), P("gx", "gy", None), P("gy", None))
    return jax.shard_map(
        local, mesh=mesh, in_specs=in_specs, out_specs=P("gy", None), check_vma=False
    )
```

```python
import functools

import jax
import jax.numpy as jnp
from jax import lax
from jax.experimental import pallas as pl
from jax.experimental.pallas import tpu as pltpu
from jax.sharding import PartitionSpec as P

F32, BF16 = jnp.float32, jnp.bfloat16
MESH = pl.DeviceIdType.MESH
C = 24
WX, WY = 32, 256
R = 10
TAPS = 2 * R + 1
MODES = 256
LANES = 128
SLAB = 384
ROW = C
NEAR = 4
CHUNKS = ((0, NEAR), (4, 3), (7, 3))


def dot(a, b):
    return jnp.dot(a, b, preferred_element_type=F32)


def split(a):
    high = a.astype(BF16)
    return high, (a - high.astype(F32)).astype(BF16)


def dot3(a, b_high, b_low):
    high, low = split(a)
    return dot(high, b_high) + (dot(high, b_low) + dot(low, b_high))


def iota(shape, dim):
    return lax.broadcasted_iota(jnp.int32, shape, dim)


def band(taps, row0, shift, shape):
    index = iota(shape, 0) - iota(shape, 1) + (row0 + shift)
    out = jnp.zeros(shape, F32)
    for j in range(TAPS):
        out = jnp.where(index == j, taps[j], out)
    return out


def kernel(
    nx, ny,
    adj_hbm, fm_hbm, tm_hbm, ke_hbm, kn_hbm, modes_hbm,
    out_ref,
    adj, modes, fm, tm, ke, kn,
    t_high, t_low, e_high, e_low, y0, ext, part,
    pack_s, pack_r, raw_s, raw_r, corner_s, corner_r, z_high, z_low, slabs, got_y, got_x,
    load_sem, ysend, yrecv, xsend, xrecv, csend, crecv, rs_send, rs_recv, ag_send, ag_recv,
):
    gx, gy = lax.axis_index("gx"), lax.axis_index("gy")
    copy_adj = pltpu.make_async_copy(adj_hbm, adj, load_sem.at[0])
    copy_kn = pltpu.make_async_copy(kn_hbm, kn, load_sem.at[1])
    copy_ke = pltpu.make_async_copy(ke_hbm, ke, load_sem.at[2])
    copy_fm = pltpu.make_async_copy(fm_hbm, fm, load_sem.at[3])
    copy_tm = pltpu.make_async_copy(tm_hbm, tm, load_sem.at[4])
    copy_modes = pltpu.make_async_copy(modes_hbm, modes, load_sem.at[5])
    for copy in (copy_adj, copy_kn, copy_ke, copy_fm, copy_tm):
        copy.start()

    barrier = pltpu.get_barrier_semaphore()

    def greet(there):
        pl.semaphore_signal(barrier, inc=1, device_id=there, device_id_type=MESH)

    west, east = jnp.maximum(gx - 1, 0), jnp.minimum(gx + 1, nx - 1)
    south, north = jnp.maximum(gy - 1, 0), jnp.minimum(gy + 1, ny - 1)
    has_x = (gx > 0, gx < nx - 1)
    has_y = (gy > 0, gy < ny - 1)
    diagonal = [
        (2 * i + j, has_x[i] & has_y[j], {"gx": (west, east)[i], "gy": (south, north)[j]})
        for i in range(2)
        for j in range(2)
    ]
    for d in range(1, nx):
        greet({"gx": gx ^ d})
    for d in range(1, ny):
        greet({"gy": gy ^ d})
    greeted = nx + ny - 2
    for i, there, device in diagonal:

        @pl.when(there)
        def _():
            greet(device)

        greeted = greeted + there.astype(jnp.int32)

    copy_kn.wait()
    for i in range(0, WY, 16):
        for h in range(0, WY, LANES):
            rows = (pl.ds(i, 16), pl.ds(h, LANES))
            if i - R > h + LANES - 1 or i + 15 + R < h:
                t_high[rows] = jnp.zeros((16, LANES), BF16)
                t_low[rows] = jnp.zeros((16, LANES), BF16)
            else:
                t_high[rows], t_low[rows] = split(band(kn, i - h, R, (16, LANES)))
    edge_row = iota((16, LANES), 0) < R
    e_high[...] = jnp.zeros_like(e_high)
    e_low[...] = jnp.zeros_like(e_low)
    low_side = jnp.where(edge_row, band(kn, 0, 0, (16, LANES)), 0.0)
    e_high[0:16, 0:LANES], e_low[0:16, 0:LANES] = split(low_side)
    high_side = jnp.where(edge_row, band(kn, WY - LANES, R, (16, LANES)), 0.0)
    e_high[16:32, LANES:WY], e_low[16:32, LANES:WY] = split(high_side)

    copy_adj.wait()
    copy_modes.start()
    lane = iota((64, LANES), 1)
    pack_low = jnp.zeros((64, LANES), F32)
    pack_high = jnp.zeros((64, LANES), F32)
    for b in range(12):
        here = (lane >= R * b) & (lane < R * (b + 1))
        low = adj[2 * b : 2 * b + 2, :, 0:LANES].reshape(64, LANES)
        high = adj[2 * b : 2 * b + 2, :, LANES:WY].reshape(64, LANES)
        if b:
            low = pltpu.roll(low, R * b, 1)
        high = pltpu.roll(high, (R * b + R) % LANES, 1)
        pack_low = jnp.where(here, low, pack_low)
        pack_high = jnp.where(here, high, pack_high)
    pack_s[0] = pack_low
    pack_s[1] = pack_high

    for side, first in enumerate((0, WX - 8)):
        for c in range(C):
            edge = adj[c, first : first + 8, :]
            for h in range(2):
                raw_s[side, h, pl.ds(c, 8, stride=ROW), :] = edge[:, LANES * h : LANES * h + LANES]

    pl.semaphore_wait(barrier, greeted)

    to_south = pltpu.make_async_remote_copy(
        pack_s.at[0], pack_r.at[1], ysend.at[0], yrecv.at[1],
        device_id={"gy": south}, device_id_type=MESH,
    )
    to_north = pltpu.make_async_remote_copy(
        pack_s.at[1], pack_r.at[0], ysend.at[1], yrecv.at[0],
        device_id={"gy": north}, device_id_type=MESH,
    )

    @pl.when(gy > 0)
    def _():
        to_south.start()

    @pl.when(gy < ny - 1)
    def _():
        to_north.start()

    near = NEAR * ROW
    raw_west = pltpu.make_async_remote_copy(
        raw_s.at[0, :, pl.ds(0, near)], raw_r.at[1], xsend.at[0], xrecv.at[0],
        device_id={"gx": west}, device_id_type=MESH,
    )
    raw_east = pltpu.make_async_remote_copy(
        raw_s.at[1, :, pl.ds(near, near)], raw_r.at[0], xsend.at[3], xrecv.at[3],
        device_id={"gx": east}, device_id_type=MESH,
    )

    @pl.when(gx > 0)
    def _():
        raw_west.start()

    @pl.when(gx < nx - 1)
    def _():
        raw_east.start()

    lane8 = iota((8, LANES), 1)
    corners = []
    for i in range(2):
        for j in range(2):
            packed = jnp.zeros((8, LANES), F32)
            for b in range(12):
                piece = raw_s[i, j, near * i + 8 * b : near * i + 8 * b + 8, :]
                piece = pltpu.roll(piece, (R * b + R * j) % LANES, 1) if b + j else piece
                packed = jnp.where((lane8 >= R * b) & (lane8 < R * (b + 1)), piece, packed)
            corner_s[2 * i + j] = packed
    for k, there, device in diagonal:
        copy = pltpu.make_async_remote_copy(
            corner_s.at[k], corner_r.at[3 - k], csend.at[k], crecv.at[3 - k],
            device_id=device, device_id_type=MESH,
        )
        corners.append(copy)

        @pl.when(there)
        def _():
            copy.start()

    for q in range(3):
        tile = adj[8 * q : 8 * q + 8].reshape(256, WY)
        y0[256 * q : 256 * q + 256, :] = dot3(tile, t_high[...], t_low[...])

    @pl.when(gy > 0)
    def _():
        to_north.wait_recv()

    @pl.when(gy == 0)
    def _():
        pack_r[0] = jnp.zeros((64, LANES), F32)

    @pl.when(gy < ny - 1)
    def _():
        to_south.wait_recv()

    @pl.when(gy == ny - 1)
    def _():
        pack_r[1] = jnp.zeros((64, LANES), F32)

    from_low, from_high = pack_r[0], pack_r[1]
    for q in range(3):
        pieces = []
        for b in range(4 * q, 4 * q + 4):
            low = pltpu.roll(from_low, (LANES - R * b) % LANES, 1) if b else from_low
            high = pltpu.roll(from_high, (LANES + 16 - R * b) % LANES, 1)
            pieces.append(jnp.where(lane < 16, low, high))
        extra = jnp.concatenate(pieces, axis=0)
        total = y0[256 * q : 256 * q + 256, :] + dot3(extra, e_high[...], e_low[...])
        for c in range(8):
            rows = pl.ds(R * ROW + 8 * q + c, WX, stride=ROW)
            ext[0, rows, :] = total[32 * c : 32 * c + 32, :LANES]
            ext[1, rows, :] = total[32 * c : 32 * c + 32, LANES:]

    to_west, to_east = [raw_west], [raw_east]
    for k, (first, count) in enumerate(CHUNKS):
        if not k:
            continue
        rows = count * ROW
        to_west.append(
            pltpu.make_async_remote_copy(
                ext.at[:, pl.ds((R + first) * ROW, rows)],
                ext.at[:, pl.ds((R + WX + first) * ROW, rows)],
                xsend.at[k], xrecv.at[k],
                device_id={"gx": west}, device_id_type=MESH,
            )
        )
        to_east.append(
            pltpu.make_async_remote_copy(
                ext.at[:, pl.ds((R + WX - first - count) * ROW, rows)],
                ext.at[:, pl.ds((R - first - count) * ROW, rows)],
                xsend.at[3 + k], xrecv.at[3 + k],
                device_id={"gx": east}, device_id_type=MESH,
            )
        )
    for k in range(1, len(CHUNKS)):

        @pl.when(gx > 0)
        def _():
            to_west[k].start()

        @pl.when(gx < nx - 1)
        def _():
            to_east[k].start()

    copy_fm.wait()
    copy_tm.wait()
    copy_ke.wait()
    row, col = iota((C, LANES), 0), iota((C, LANES), 1)
    field_part = jnp.zeros((C, LANES), F32)
    for g in range(4):
        for f in range(4):
            chosen = (row // 6 == g) & (col // 6 == f)
            field_part = jnp.where(chosen, fm[g, f], field_part)
    time_part = jnp.zeros((C, LANES), F32)
    for s in range(6):
        for t in range(6):
            chosen = (row % 6 == s) & (col % 6 == t)
            time_part = jnp.where(chosen, tm[s, t], time_part)
    mix = field_part * time_part
    group = lax.rem(gy, 8)
    lane_of = iota((SLAB, C), 0)
    channel = 8 * (lane_of // LANES) + lax.rem(group + 8 - (lane_of % LANES) // 16, 8)
    pick = (channel == iota((SLAB, C), 1)).astype(F32)
    mixing = jnp.dot(pick, mix, preferred_element_type=F32, precision=lax.Precision.HIGHEST)
    z_high[...], z_low[...] = split(mixing)

    def column(start):
        return jnp.concatenate([ext[h, pl.ds(start, ROW), :] for h in range(2)], axis=1)

    def columns(start, count, first_tap):
        total = ke[first_tap] * column(start)
        for j in range(1, count):
            total = total + ke[first_tap + j] * column(start + j * ROW)
        return total

    def project(total, x):
        low = total - total.astype(BF16).astype(F32)
        both = jnp.concatenate([total, low], axis=0).astype(BF16)
        return dot(both, modes[x])

    copy_modes.wait()

    def interior(x, acc):
        start = pl.multiple_of(x * ROW, 8)
        return acc + project(columns(start, TAPS, 0), x)

    acc = lax.fori_loop(R, WX - R, interior, jnp.zeros((2 * C, MODES), F32))

    for e in range(R):
        part[e] = columns(R * ROW, e + R + 1, R - e)
        part[R + e] = columns((WX - 1 - e) * ROW, e + R + 1, 0)

    @pl.when(gx == 0)
    def _():
        ext[:, 0 : R * ROW, :] = jnp.zeros((2, R * ROW, LANES), F32)

    @pl.when(gx == nx - 1)
    def _():
        ext[:, (R + WX) * ROW : (2 * R + WX) * ROW, :] = jnp.zeros((2, R * ROW, LANES), F32)

    for k, (first, count) in enumerate(CHUNKS):

        @pl.when(gx > 0)
        def _():
            to_east[k].wait_recv()

        @pl.when(gx < nx - 1)
        def _():
            to_west[k].wait_recv()

        if not k:
            for i, there, device in diagonal:

                @pl.when(there)
                def _():
                    corners[3 - i].wait_recv()

                @pl.when(jnp.logical_not(there))
                def _():
                    corner_r[i] = jnp.zeros((8, LANES), F32)

            for side in range(2):

                @pl.when(has_x[side])
                def _():
                    low, high = corner_r[2 * side], corner_r[2 * side + 1]
                    pieces = []
                    for b in range(12):
                        a = pltpu.roll(low, (LANES - R * b) % LANES, 1) if b else low
                        c = pltpu.roll(high, (LANES + 16 - R * b) % LANES, 1)
                        pieces.append(jnp.where(lane8 < 16, a, c))
                    extra = jnp.concatenate(pieces, axis=0)
                    tile = jnp.concatenate([raw_r[side, 0], raw_r[side, 1]], axis=1)
                    done = dot3(tile, t_high[...], t_low[...])
                    done = done + dot3(extra, e_high[...], e_low[...])
                    at = (R - NEAR) * ROW if side == 0 else (R + WX) * ROW
                    ext[0, pl.ds(at, near), :] = done[:, :LANES]
                    ext[1, pl.ds(at, near), :] = done[:, LANES:]

        last = first + count
        for e in range(R - first):
            low, high = part[e], part[R + e]
            for d in range(first + 1, min(last, R - e) + 1):
                low = low + ke[R - d - e] * column((R - d) * ROW)
                high = high + ke[R + d + e] * column((R + WX - 1 + d) * ROW)
            if R - e <= last:
                acc = acc + project(low, e)
                acc = acc + project(high, WX - 1 - e)
            else:
                part[e] = low
                part[R + e] = high

    total = acc[:C] + acc[C:]

    sub, lanes = iota((8, LANES), 0), iota((8, LANES), 1) // 16
    for r in range(3):
        for h in range(2):
            v = total[8 * r : 8 * r + 8, LANES * h : LANES * h + LANES]
            for bit in (1, 2, 4):
                v = jnp.where((sub & bit) != 0, pltpu.roll(v, LANES - 16 * bit, 1), v)
            for bit in (1, 2, 4):
                v = jnp.where((lanes & bit) != 0, pltpu.roll(v, bit, 0), v)
            for g in range(8):
                slabs[8 * h + g, :, LANES * r : LANES * r + LANES] = v[g : g + 1]

    for d in sorted(range(1, ny), key=lambda d: -2 * (d & 12).bit_count() - (d & 3).bit_count()):
        peer = gy ^ d
        pltpu.make_async_remote_copy(
            slabs.at[peer], got_y.at[d - 1], rs_send, rs_recv,
            device_id={"gy": peer}, device_id_type=MESH,
        ).start()

    mine = slabs[gy]
    pltpu.make_async_copy(got_y, got_y, rs_recv).wait()
    for d in range(ny - 1):
        mine = mine + got_y[d]
    got_x[gx] = mine

    for peer in range(nx):

        @pl.when(gx != peer)
        def _():
            pltpu.make_async_remote_copy(
                got_x.at[gx], got_x.at[gx], ag_send, ag_recv,
                device_id={"gx": peer}, device_id_type=MESH,
            ).start()

    others = got_x.at[pl.ds(0, nx - 1)]
    pltpu.make_async_copy(others, others, ag_recv).wait()
    whole = got_x[0]
    for d in range(1, nx):
        whole = whole + got_x[d]

    shape = (16, SLAB)
    spread = jnp.where(
        iota(shape, 1) % 16 == iota(shape, 0), jnp.broadcast_to(whole, shape), 0.0
    )
    out_ref[...] = dot3(spread, z_high[...], z_low[...])[:, :C]

    @pl.when(gy > 0)
    def _():
        to_south.wait_send()

    @pl.when(gy < ny - 1)
    def _():
        to_north.wait_send()

    for k in range(len(CHUNKS)):

        @pl.when(gx > 0)
        def _():
            to_west[k].wait_send()

        @pl.when(gx < nx - 1)
        def _():
            to_east[k].wait_send()

    for k, there, device in diagonal:

        @pl.when(there)
        def _():
            corners[k].wait_send()

    pltpu.make_async_copy(got_y, got_y, rs_send).wait()
    pltpu.make_async_copy(others, others, ag_send).wait()


def solution(mesh):
    nx, ny = mesh.shape["gx"], mesh.shape["gy"]

    def local(adj, field_mixing, time_mixing, kernel_east, kernel_north, modes, coefficients):
        vmem, smem, dma = pltpu.VMEM, pltpu.SMEM, pltpu.SemaphoreType.DMA
        operands = (
            adj.reshape(C, WX, WY), field_mixing, time_mixing, kernel_east, kernel_north, modes
        )
        projection = pl.pallas_call(
            functools.partial(kernel, nx, ny),
            out_shape=jax.ShapeDtypeStruct((MODES // ny, C), F32),
            in_specs=[pl.BlockSpec(memory_space=pltpu.HBM)] * 6,
            out_specs=pl.BlockSpec(memory_space=pltpu.VMEM),
            scratch_shapes=[
                vmem((C, WX, WY), F32),
                vmem((WX, WY, MODES), BF16),
                smem((4, 4), F32),
                smem((6, 6), F32),
                smem((TAPS,), F32),
                smem((TAPS,), F32),
                vmem((WY, WY), BF16),
                vmem((WY, WY), BF16),
                vmem((LANES, WY), BF16),
                vmem((LANES, WY), BF16),
                vmem((C * WX, WY), F32),
                vmem((2, (WX + 2 * R) * ROW, LANES), F32),
                vmem((2 * R, C, WY), F32),
                vmem((2, 64, LANES), F32),
                vmem((2, 64, LANES), F32),
                vmem((2, 2, 8 * ROW, LANES), F32),
                vmem((2, 2, NEAR * ROW, LANES), F32),
                vmem((4, 8, LANES), F32),
                vmem((4, 8, LANES), F32),
                vmem((SLAB, LANES), BF16),
                vmem((SLAB, LANES), BF16),
                vmem((ny, 1, SLAB), F32),
                vmem((ny - 1, 1, SLAB), F32),
                vmem((nx, 1, SLAB), F32),
                dma((6,)),
                dma((2,)),
                dma((2,)),
                dma((6,)),
                dma((6,)),
                dma((4,)),
                dma((4,)),
                dma,
                dma,
                dma,
                dma,
            ],
            compiler_params=pltpu.CompilerParams(
                collective_id=0, has_side_effects=True, vmem_limit_bytes=40 << 20
            ),
            name="gradient",
        )(*[pltpu.with_memory_space_constraint(a, pltpu.HBM) for a in operands])
        return coefficients + projection

    in_specs = (P(None, None, "gx", "gy"), P(), P(), P(), P(), P("gx", "gy", None), P("gy", None))
    return jax.shard_map(
        local, mesh=mesh, in_specs=in_specs, out_specs=P("gy", None), check_vma=False
    )
```

```python
import functools

import jax
import jax.numpy as jnp
from jax import lax
from jax.experimental import pallas as pl
from jax.experimental.pallas import tpu as pltpu
from jax.sharding import PartitionSpec as P

F32, BF16 = jnp.float32, jnp.bfloat16
MESH = pl.DeviceIdType.MESH
C = 24
WX, WY = 32, 256
R = 10
TAPS = 2 * R + 1
MODES = 256
LANES = 128
SLAB = 384
ROW = C
NEAR = 4
CHUNKS = ((0, NEAR), (4, 4), (8, 2))


def dot(a, b):
    return jnp.dot(a, b, preferred_element_type=F32)


def split(a):
    high = a.astype(BF16)
    return high, (a - high.astype(F32)).astype(BF16)


def dot3(a, b_high, b_low):
    high, low = split(a)
    return dot(high, b_high) + (dot(high, b_low) + dot(low, b_high))


def iota(shape, dim):
    return lax.broadcasted_iota(jnp.int32, shape, dim)


def band(taps, row0, shift, shape):
    index = iota(shape, 0) - iota(shape, 1) + (row0 + shift)
    out = jnp.zeros(shape, F32)
    for j in range(TAPS):
        out = jnp.where(index == j, taps[j], out)
    return out


def kernel(
    nx, ny,
    adj_hbm, fm_hbm, tm_hbm, ke_hbm, kn_hbm, modes_hbm,
    out_ref,
    adj, modes, fm, tm, ke, kn,
    t_high, t_low, e_high, e_low, y0, ext, part,
    pack_s, pack_r, raw_s, raw_r, corner_s, corner_r, z_high, z_low, slabs, got_y, got_x,
    load_sem, ysend, yrecv, xsend, xrecv, csend, crecv, rs_send, rs_recv, ag_send, ag_recv,
):
    gx, gy = lax.axis_index("gx"), lax.axis_index("gy")
    copy_adj = pltpu.make_async_copy(adj_hbm, adj, load_sem.at[0])
    copy_kn = pltpu.make_async_copy(kn_hbm, kn, load_sem.at[1])
    copy_ke = pltpu.make_async_copy(ke_hbm, ke, load_sem.at[2])
    copy_fm = pltpu.make_async_copy(fm_hbm, fm, load_sem.at[3])
    copy_tm = pltpu.make_async_copy(tm_hbm, tm, load_sem.at[4])
    copy_modes = pltpu.make_async_copy(modes_hbm, modes, load_sem.at[5])
    for copy in (copy_adj, copy_kn, copy_ke, copy_fm, copy_tm):
        copy.start()

    barrier = pltpu.get_barrier_semaphore()

    def greet(there):
        pl.semaphore_signal(barrier, inc=1, device_id=there, device_id_type=MESH)

    west, east = jnp.maximum(gx - 1, 0), jnp.minimum(gx + 1, nx - 1)
    south, north = jnp.maximum(gy - 1, 0), jnp.minimum(gy + 1, ny - 1)
    has_x = (gx > 0, gx < nx - 1)
    has_y = (gy > 0, gy < ny - 1)
    diagonal = [
        (2 * i + j, has_x[i] & has_y[j], {"gx": (west, east)[i], "gy": (south, north)[j]})
        for i in range(2)
        for j in range(2)
    ]
    for d in sorted(range(1, nx), key=lambda d: -min(d // 2, nx // 2 - d // 2)):
        greet({"gx": gx ^ d})
    for d in sorted(range(1, ny), key=lambda d: -2 * (d & 12).bit_count() - (d & 3).bit_count()):
        greet({"gy": gy ^ d})
    greeted = nx + ny - 2
    for i, there, device in diagonal:

        @pl.when(there)
        def _():
            greet(device)

        greeted = greeted + there.astype(jnp.int32)

    copy_kn.wait()
    for i in range(0, WY, 16):
        for h in range(0, WY, LANES):
            rows = (pl.ds(i, 16), pl.ds(h, LANES))
            if i - R > h + LANES - 1 or i + 15 + R < h:
                t_high[rows] = jnp.zeros((16, LANES), BF16)
                t_low[rows] = jnp.zeros((16, LANES), BF16)
            else:
                t_high[rows], t_low[rows] = split(band(kn, i - h, R, (16, LANES)))
    edge_row = iota((16, LANES), 0) < R
    e_high[...] = jnp.zeros_like(e_high)
    e_low[...] = jnp.zeros_like(e_low)
    low_side = jnp.where(edge_row, band(kn, 0, 0, (16, LANES)), 0.0)
    e_high[0:16, 0:LANES], e_low[0:16, 0:LANES] = split(low_side)
    high_side = jnp.where(edge_row, band(kn, WY - LANES, R, (16, LANES)), 0.0)
    e_high[16:32, LANES:WY], e_low[16:32, LANES:WY] = split(high_side)

    copy_adj.wait()
    copy_modes.start()
    lane = iota((64, LANES), 1)
    pack_low = jnp.zeros((64, LANES), F32)
    pack_high = jnp.zeros((64, LANES), F32)
    for b in range(12):
        here = (lane >= R * b) & (lane < R * (b + 1))
        low = adj[2 * b : 2 * b + 2, :, 0:LANES].reshape(64, LANES)
        high = adj[2 * b : 2 * b + 2, :, LANES:WY].reshape(64, LANES)
        if b:
            low = pltpu.roll(low, R * b, 1)
        high = pltpu.roll(high, (R * b + R) % LANES, 1)
        pack_low = jnp.where(here, low, pack_low)
        pack_high = jnp.where(here, high, pack_high)
    pack_s[0] = pack_low
    pack_s[1] = pack_high

    for side, first in enumerate((0, WX - 8)):
        for c in range(C):
            edge = adj[c, first : first + 8, :]
            for h in range(2):
                raw_s[side, h, pl.ds(c, 8, stride=ROW), :] = edge[:, LANES * h : LANES * h + LANES]

    pl.semaphore_wait(barrier, greeted)

    to_south = pltpu.make_async_remote_copy(
        pack_s.at[0], pack_r.at[1], ysend.at[0], yrecv.at[1],
        device_id={"gy": south}, device_id_type=MESH,
    )
    to_north = pltpu.make_async_remote_copy(
        pack_s.at[1], pack_r.at[0], ysend.at[1], yrecv.at[0],
        device_id={"gy": north}, device_id_type=MESH,
    )

    @pl.when(gy > 0)
    def _():
        to_south.start()

    @pl.when(gy < ny - 1)
    def _():
        to_north.start()

    near = NEAR * ROW
    raw_west = pltpu.make_async_remote_copy(
        raw_s.at[0, :, pl.ds(0, near)], raw_r.at[1], xsend.at[0], xrecv.at[0],
        device_id={"gx": west}, device_id_type=MESH,
    )
    raw_east = pltpu.make_async_remote_copy(
        raw_s.at[1, :, pl.ds(near, near)], raw_r.at[0], xsend.at[3], xrecv.at[3],
        device_id={"gx": east}, device_id_type=MESH,
    )

    @pl.when(gx > 0)
    def _():
        raw_west.start()

    @pl.when(gx < nx - 1)
    def _():
        raw_east.start()

    lane8 = iota((8, LANES), 1)
    corners = []
    for i in range(2):
        for j in range(2):
            packed = jnp.zeros((8, LANES), F32)
            for b in range(12):
                piece = raw_s[i, j, near * i + 8 * b : near * i + 8 * b + 8, :]
                piece = pltpu.roll(piece, (R * b + R * j) % LANES, 1) if b + j else piece
                packed = jnp.where((lane8 >= R * b) & (lane8 < R * (b + 1)), piece, packed)
            corner_s[2 * i + j] = packed
    for k, there, device in diagonal:
        copy = pltpu.make_async_remote_copy(
            corner_s.at[k], corner_r.at[3 - k], csend.at[k], crecv.at[3 - k],
            device_id=device, device_id_type=MESH,
        )
        corners.append(copy)

        @pl.when(there)
        def _():
            copy.start()

    for q in range(3):
        tile = adj[8 * q : 8 * q + 8].reshape(256, WY)
        y0[256 * q : 256 * q + 256, :] = dot3(tile, t_high[...], t_low[...])

    @pl.when(gy > 0)
    def _():
        to_north.wait_recv()

    @pl.when(gy == 0)
    def _():
        pack_r[0] = jnp.zeros((64, LANES), F32)

    @pl.when(gy < ny - 1)
    def _():
        to_south.wait_recv()

    @pl.when(gy == ny - 1)
    def _():
        pack_r[1] = jnp.zeros((64, LANES), F32)

    from_low, from_high = pack_r[0], pack_r[1]
    for q in range(3):
        pieces = []
        for b in range(4 * q, 4 * q + 4):
            low = pltpu.roll(from_low, (LANES - R * b) % LANES, 1) if b else from_low
            high = pltpu.roll(from_high, (LANES + 16 - R * b) % LANES, 1)
            pieces.append(jnp.where(lane < 16, low, high))
        extra = jnp.concatenate(pieces, axis=0)
        total = y0[256 * q : 256 * q + 256, :] + dot3(extra, e_high[...], e_low[...])
        for c in range(8):
            rows = pl.ds(R * ROW + 8 * q + c, WX, stride=ROW)
            ext[0, rows, :] = total[32 * c : 32 * c + 32, :LANES]
            ext[1, rows, :] = total[32 * c : 32 * c + 32, LANES:]

    to_west, to_east = [raw_west], [raw_east]
    for k, (first, count) in enumerate(CHUNKS):
        if not k:
            continue
        rows = count * ROW
        to_west.append(
            pltpu.make_async_remote_copy(
                ext.at[:, pl.ds((R + first) * ROW, rows)],
                ext.at[:, pl.ds((R + WX + first) * ROW, rows)],
                xsend.at[k], xrecv.at[k],
                device_id={"gx": west}, device_id_type=MESH,
            )
        )
        to_east.append(
            pltpu.make_async_remote_copy(
                ext.at[:, pl.ds((R + WX - first - count) * ROW, rows)],
                ext.at[:, pl.ds((R - first - count) * ROW, rows)],
                xsend.at[3 + k], xrecv.at[3 + k],
                device_id={"gx": east}, device_id_type=MESH,
            )
        )
    for k in range(1, len(CHUNKS)):

        @pl.when(gx > 0)
        def _():
            to_west[k].start()

        @pl.when(gx < nx - 1)
        def _():
            to_east[k].start()

    copy_fm.wait()
    copy_tm.wait()
    copy_ke.wait()
    row, col = iota((C, LANES), 0), iota((C, LANES), 1)
    field_part = jnp.zeros((C, LANES), F32)
    for g in range(4):
        for f in range(4):
            chosen = (row // 6 == g) & (col // 6 == f)
            field_part = jnp.where(chosen, fm[g, f], field_part)
    time_part = jnp.zeros((C, LANES), F32)
    for s in range(6):
        for t in range(6):
            chosen = (row % 6 == s) & (col % 6 == t)
            time_part = jnp.where(chosen, tm[s, t], time_part)
    mix = field_part * time_part
    group = lax.rem(gy, 8)
    lane_of = iota((SLAB, C), 0)
    channel = 8 * (lane_of // LANES) + lax.rem(group + 8 - (lane_of % LANES) // 16, 8)
    pick = (channel == iota((SLAB, C), 1)).astype(F32)
    mixing = jnp.dot(pick, mix, preferred_element_type=F32, precision=lax.Precision.HIGHEST)
    z_high[...], z_low[...] = split(mixing)

    def column(start):
        return jnp.concatenate([ext[h, pl.ds(start, ROW), :] for h in range(2)], axis=1)

    def columns(start, count, first_tap):
        total = ke[first_tap] * column(start)
        for j in range(1, count):
            total = total + ke[first_tap + j] * column(start + j * ROW)
        return total

    def project(total, x):
        low = total - total.astype(BF16).astype(F32)
        both = jnp.concatenate([total, low], axis=0).astype(BF16)
        return dot(both, modes[x])

    copy_modes.wait()

    def interior(x, acc):
        start = pl.multiple_of(x * ROW, 8)
        return acc + project(columns(start, TAPS, 0), x)

    acc = lax.fori_loop(R, WX - R, interior, jnp.zeros((2 * C, MODES), F32))

    for e in range(R):
        part[e] = columns(R * ROW, e + R + 1, R - e)
        part[R + e] = columns((WX - 1 - e) * ROW, e + R + 1, 0)

    @pl.when(gx == 0)
    def _():
        ext[:, 0 : R * ROW, :] = jnp.zeros((2, R * ROW, LANES), F32)

    @pl.when(gx == nx - 1)
    def _():
        ext[:, (R + WX) * ROW : (2 * R + WX) * ROW, :] = jnp.zeros((2, R * ROW, LANES), F32)

    for k, (first, count) in enumerate(CHUNKS):

        @pl.when(gx > 0)
        def _():
            to_east[k].wait_recv()

        @pl.when(gx < nx - 1)
        def _():
            to_west[k].wait_recv()

        if not k:
            for i, there, device in diagonal:

                @pl.when(there)
                def _():
                    corners[3 - i].wait_recv()

                @pl.when(jnp.logical_not(there))
                def _():
                    corner_r[i] = jnp.zeros((8, LANES), F32)

            for side in range(2):

                @pl.when(has_x[side])
                def _():
                    low, high = corner_r[2 * side], corner_r[2 * side + 1]
                    pieces = []
                    for b in range(12):
                        a = pltpu.roll(low, (LANES - R * b) % LANES, 1) if b else low
                        c = pltpu.roll(high, (LANES + 16 - R * b) % LANES, 1)
                        pieces.append(jnp.where(lane8 < 16, a, c))
                    extra = jnp.concatenate(pieces, axis=0)
                    tile = jnp.concatenate([raw_r[side, 0], raw_r[side, 1]], axis=1)
                    done = dot3(tile, t_high[...], t_low[...])
                    done = done + dot3(extra, e_high[...], e_low[...])
                    at = (R - NEAR) * ROW if side == 0 else (R + WX) * ROW
                    ext[0, pl.ds(at, near), :] = done[:, :LANES]
                    ext[1, pl.ds(at, near), :] = done[:, LANES:]

        last = first + count
        for e in range(R - first):
            low, high = part[e], part[R + e]
            for d in range(first + 1, min(last, R - e) + 1):
                low = low + ke[R - d - e] * column((R - d) * ROW)
                high = high + ke[R + d + e] * column((R + WX - 1 + d) * ROW)
            if R - e <= last:
                acc = acc + project(low, e)
                acc = acc + project(high, WX - 1 - e)
            else:
                part[e] = low
                part[R + e] = high

    total = acc[:C] + acc[C:]

    sub, lanes = iota((8, LANES), 0), iota((8, LANES), 1) // 16
    for r in range(3):
        for h in range(2):
            v = total[8 * r : 8 * r + 8, LANES * h : LANES * h + LANES]
            for bit in (1, 2, 4):
                v = jnp.where((sub & bit) != 0, pltpu.roll(v, LANES - 16 * bit, 1), v)
            for bit in (1, 2, 4):
                v = jnp.where((lanes & bit) != 0, pltpu.roll(v, bit, 0), v)
            for g in range(8):
                slabs[8 * h + g, :, LANES * r : LANES * r + LANES] = v[g : g + 1]

    for d in sorted(range(1, ny), key=lambda d: -2 * (d & 12).bit_count() - (d & 3).bit_count()):
        peer = gy ^ d
        pltpu.make_async_remote_copy(
            slabs.at[peer], got_y.at[d - 1], rs_send, rs_recv,
            device_id={"gy": peer}, device_id_type=MESH,
        ).start()

    mine = slabs[gy]
    pltpu.make_async_copy(got_y, got_y, rs_recv).wait()
    for d in range(ny - 1):
        mine = mine + got_y[d]
    got_x[gx] = mine

    for peer in range(nx):

        @pl.when(gx != peer)
        def _():
            pltpu.make_async_remote_copy(
                got_x.at[gx], got_x.at[gx], ag_send, ag_recv,
                device_id={"gx": peer}, device_id_type=MESH,
            ).start()

    others = got_x.at[pl.ds(0, nx - 1)]
    pltpu.make_async_copy(others, others, ag_recv).wait()
    whole = got_x[0]
    for d in range(1, nx):
        whole = whole + got_x[d]

    shape = (16, SLAB)
    spread = jnp.where(
        iota(shape, 1) % 16 == iota(shape, 0), jnp.broadcast_to(whole, shape), 0.0
    )
    out_ref[...] = dot3(spread, z_high[...], z_low[...])[:, :C]

    @pl.when(gy > 0)
    def _():
        to_south.wait_send()

    @pl.when(gy < ny - 1)
    def _():
        to_north.wait_send()

    for k in range(len(CHUNKS)):

        @pl.when(gx > 0)
        def _():
            to_west[k].wait_send()

        @pl.when(gx < nx - 1)
        def _():
            to_east[k].wait_send()

    for k, there, device in diagonal:

        @pl.when(there)
        def _():
            corners[k].wait_send()

    pltpu.make_async_copy(got_y, got_y, rs_send).wait()
    pltpu.make_async_copy(others, others, ag_send).wait()


def solution(mesh):
    nx, ny = mesh.shape["gx"], mesh.shape["gy"]

    def local(adj, field_mixing, time_mixing, kernel_east, kernel_north, modes, coefficients):
        vmem, smem, dma = pltpu.VMEM, pltpu.SMEM, pltpu.SemaphoreType.DMA
        operands = (
            adj.reshape(C, WX, WY), field_mixing, time_mixing, kernel_east, kernel_north, modes
        )
        projection = pl.pallas_call(
            functools.partial(kernel, nx, ny),
            out_shape=jax.ShapeDtypeStruct((MODES // ny, C), F32),
            in_specs=[pl.BlockSpec(memory_space=pltpu.HBM)] * 6,
            out_specs=pl.BlockSpec(memory_space=pltpu.VMEM),
            scratch_shapes=[
                vmem((C, WX, WY), F32),
                vmem((WX, WY, MODES), BF16),
                smem((4, 4), F32),
                smem((6, 6), F32),
                smem((TAPS,), F32),
                smem((TAPS,), F32),
                vmem((WY, WY), BF16),
                vmem((WY, WY), BF16),
                vmem((LANES, WY), BF16),
                vmem((LANES, WY), BF16),
                vmem((C * WX, WY), F32),
                vmem((2, (WX + 2 * R) * ROW, LANES), F32),
                vmem((2 * R, C, WY), F32),
                vmem((2, 64, LANES), F32),
                vmem((2, 64, LANES), F32),
                vmem((2, 2, 8 * ROW, LANES), F32),
                vmem((2, 2, NEAR * ROW, LANES), F32),
                vmem((4, 8, LANES), F32),
                vmem((4, 8, LANES), F32),
                vmem((SLAB, LANES), BF16),
                vmem((SLAB, LANES), BF16),
                vmem((ny, 1, SLAB), F32),
                vmem((ny - 1, 1, SLAB), F32),
                vmem((nx, 1, SLAB), F32),
                dma((6,)),
                dma((2,)),
                dma((2,)),
                dma((6,)),
                dma((6,)),
                dma((4,)),
                dma((4,)),
                dma,
                dma,
                dma,
                dma,
            ],
            compiler_params=pltpu.CompilerParams(
                collective_id=0, has_side_effects=True, vmem_limit_bytes=40 << 20
            ),
            name="gradient",
        )(*[pltpu.with_memory_space_constraint(a, pltpu.HBM) for a in operands])
        return coefficients + projection

    in_specs = (P(None, None, "gx", "gy"), P(), P(), P(), P(), P("gx", "gy", None), P("gy", None))
    return jax.shard_map(
        local, mesh=mesh, in_specs=in_specs, out_specs=P("gy", None), check_vma=False
    )
```
